128 devices in a mesh: src: 4 (over y), row: 32 (over x, z, core).
Axes of the slice: x: 4, y: 4, z: 4, core: 2. Of those that a mesh axis runs over, the one named last changes fastest.
Arguments:
- load_root: bfloat16 [8192, 1536], P('row', 'src'), may hold values from -48 to 48
- load_branch: bfloat16 [2, 8192, 1536], P(None, 'row', 'src'), may hold values from -48 to 48
- load_leaf: bfloat16 [4, 4096, 1536], P(None, 'row', 'src'), may hold values from -48 to 48
- inverse_root: bfloat16 [8192, 8192], P('row'), may hold values from -1.5 to 1.5, as said below
- inverse_branch: bfloat16 [2, 8192, 8192], P(None, 'row'), may hold values from -1.5 to 1.5, as said below
- inverse_leaf: bfloat16 [4, 4096, 4096], P(None, 'row'), may hold values from -1.5 to 1.5, as said below
- coupling_branch: bfloat16 [2, 2048, 8192], P(None, None, 'row'), may hold values from -0.0625 to 0.0625
- coupling_leaf: bfloat16 [4, 2048, 4096], P(None, None, 'row'), may hold values from -0.09375 to 0.09375
- blocks_branch: int32 [2, 16], replicated, may hold values from 0 to 63, as said below
- blocks_leaf: int32 [4, 16], replicated, may hold values from 0 to 127, as said below
- parents: int32 [4], replicated, may hold values from 0 to 1, as said below
Outputs:
- field_root: float32 [8192, 1536], P('row', 'src')
- field_branch: float32 [2, 8192, 1536], P(None, 'row', 'src')
- field_leaf: float32 [4, 4096, 1536], P(None, 'row', 'src')
- coverage_root: float32 [8192], P('row')
- coverage_branch: float32 [2, 8192], P(None, 'row')
- coverage_leaf: float32 [4, 4096], P(None, 'row')
The draws below stay inside these ranges and needn't reach their ends.
Inputs may be any that keep to these rules, and one draw needn't show every extreme that they name: `inverse_root`: lower triangular; diagonal entries between 0.5 and 1.5. `inverse_branch`: each block lower triangular; diagonal entries between 0.5 and 1.5. `inverse_leaf`: each block lower triangular; diagonal entries between 0.5 and 1.5. `blocks_branch`: each row holds distinct root block numbers. `blocks_leaf`: each row holds distinct numbers; its first 8 entries are below 8192/128 (parent blocks), the others are 64 or more (root blocks). `parents`: each of the two level-1 separators is the parent of exactly two level-2 separators.
All inputs are finite; a program needn't handle non-finite values.
Results may differ from the reference program's by a relative error of at most 0.0055.
Values may be sent and summed in bfloat16 or wider, within the bound.
A program may use at most 128 MiB of HBM per device.

```python
import math
import jax
import jax.numpy as jnp
from jax import lax

ROOT_ROWS = 8192
BRANCH_ROWS = 8192
LEAF_ROWS = 4096
COUPLE_ROWS = 2048
BLOCK_ROWS = 128
SOURCES = 1536
COUPLE_BLOCKS = 16


def load_draw(key, extent):
    key_values, key_spread = jax.random.split(key, 2)
    position = jnp.arange(extent[-1], dtype=jnp.float32) / extent[-1]
    values = jax.random.truncated_normal(key_values, -5.0, 5.0, extent, jnp.float32)
    growth = jnp.exp(jnp.log(3.0) * position)
    spread = jax.random.uniform(key_spread, (extent[-1],), jnp.float32, 0.7, 1.4)
    return (values * growth * spread).astype(jnp.bfloat16)


def inverse_draw(key, node_count, width):
    key_lower, key_diagonal = jax.random.split(key, 2)
    row_ids = jnp.arange(width)[:, None]
    col_ids = jnp.arange(width)[None, :]
    values = jax.random.truncated_normal(key_lower, -5.0, 5.0, (node_count, width, width), jnp.float32)
    values = values * (1.5 / math.sqrt(width))
    diagonal = jax.random.uniform(key_diagonal, (node_count, width, 1), jnp.float32, 0.5, 1.5)
    result = jnp.where(row_ids > col_ids, values, 0.0) + jnp.where(row_ids == col_ids, diagonal, 0.0)
    return result.astype(jnp.bfloat16)


def draw_load_root(key, part):
    return load_draw(key, (ROOT_ROWS, SOURCES))


def draw_load_branch(key, part):
    return load_draw(key, (2, BRANCH_ROWS, SOURCES))


def draw_load_leaf(key, part):
    return load_draw(key, (4, LEAF_ROWS, SOURCES))


def draw_inverse_root(key, part):
    return inverse_draw(key, 1, ROOT_ROWS)[0]


def draw_inverse_branch(key, part):
    return inverse_draw(key, 2, BRANCH_ROWS)


def draw_inverse_leaf(key, part):
    return inverse_draw(key, 4, LEAF_ROWS)


def draw_parents(key, part):
    order = jax.random.permutation(jax.random.fold_in(key, 11), 4)
    return (order // 2).astype(jnp.int32)


def draw_blocks_leaf(key, part):
    key_list = jax.random.split(jax.random.fold_in(key, 12), 8)
    half_count = COUPLE_BLOCKS // 2
    branch_blocks = BRANCH_ROWS // BLOCK_ROWS
    lower_part = jnp.stack([jax.random.permutation(key_list[i], branch_blocks)[:half_count] for i in range(4)])
    upper_part = jnp.stack([branch_blocks + jax.random.permutation(key_list[4 + i], ROOT_ROWS // BLOCK_ROWS)[:half_count] for i in range(4)])
    return jnp.concatenate([lower_part, upper_part], axis=1).astype(jnp.int32)


def draw_blocks_branch(key, part):
    key_list = jax.random.split(jax.random.fold_in(key, 13), 2)
    return jnp.stack([jax.random.permutation(key_list[i], ROOT_ROWS // BLOCK_ROWS)[:COUPLE_BLOCKS] for i in range(2)]).astype(jnp.int32)


def levels(own_key, shape, shards, low, high):
    factor_of = 1.0
    for dim, shards_of in shards:
        draws = jax.random.uniform(jax.random.fold_in(jax.random.fold_in(own_key, 6), dim), (shards_of,), jnp.float32, low / len(shards), high / len(shards))
        factor_of = factor_of * jnp.repeat(jnp.exp(draws), shape[dim] // shards_of).reshape((-1,) + (1,) * (len(shape) - 1 - dim))
    return factor_of


def gaussian(own_key, shape, deviation, bound, cuts=(), held_as=jnp.bfloat16):
    values = jax.random.normal(own_key, shape, jnp.float32) * deviation
    if len(cuts) > 0:
        values = levels(own_key, shape, cuts, -0.22, 0.18) * values
    return jnp.clip(values, min=-bound, max=bound).astype(held_as)


def setup_inputs(seed: int = 0) -> dict:
    keys = jax.random.split(jax.random.key(seed), 12)
    load_root = draw_load_root(jax.random.fold_in(keys[11], 71), 0)
    load_branch = draw_load_branch(jax.random.fold_in(keys[11], 71), 0)
    load_leaf = draw_load_leaf(jax.random.fold_in(keys[11], 71), 0)
    inverse_root = draw_inverse_root(jax.random.fold_in(keys[11], 71), 0)
    inverse_branch = draw_inverse_branch(jax.random.fold_in(keys[11], 71), 0)
    inverse_leaf = draw_inverse_leaf(jax.random.fold_in(keys[11], 71), 0)
    coupling_branch = gaussian(keys[6], (2, COUPLE_ROWS, BRANCH_ROWS), BRANCH_ROWS ** -0.5, 0.0625, ((2, 32),))
    coupling_leaf = gaussian(keys[7], (4, COUPLE_ROWS, LEAF_ROWS), LEAF_ROWS ** -0.5, 0.09375, ((2, 32),))
    blocks_branch = draw_blocks_branch(jax.random.fold_in(keys[11], 71), 0)
    blocks_leaf = draw_blocks_leaf(jax.random.fold_in(keys[11], 71), 0)
    parents = draw_parents(jax.random.fold_in(keys[11], 71), 0)
    return {"load_root": load_root, "load_branch": load_branch, "load_leaf": load_leaf, "inverse_root": inverse_root, "inverse_branch": inverse_branch, "inverse_leaf": inverse_leaf, "coupling_branch": coupling_branch, "coupling_leaf": coupling_leaf, "blocks_branch": blocks_branch, "blocks_leaf": blocks_leaf, "parents": parents}


def place_blocks(values, node_ids, blocks, block_count, node_total):
    target = node_ids * block_count + blocks
    buckets = jnp.zeros((node_total * block_count,) + values.shape[1:], jnp.float32)
    buckets = buckets.at[target].add(values)
    return buckets.reshape(node_total, block_count * values.shape[1], values.shape[2])


def solve_level(inverse, loads):
    return jnp.einsum("nrw,nwc->nrc", inverse.astype(jnp.float32), loads.astype(jnp.float32),
                      precision=lax.Precision.HIGHEST)


def reference(load_root, load_branch, load_leaf, inverse_root, inverse_branch, inverse_leaf,
              coupling_branch, coupling_leaf, blocks_branch, blocks_leaf, parents):
    source_count = load_leaf.shape[2]
    half_count = COUPLE_BLOCKS // 2
    branch_blocks = BRANCH_ROWS // BLOCK_ROWS
    root_blocks = ROOT_ROWS // BLOCK_ROWS
    field_leaf = solve_level(inverse_leaf, load_leaf)
    leaf_z = field_leaf.astype(jnp.bfloat16)
    leaf_u = jnp.einsum("nrw,nwc->nrc", coupling_leaf.astype(jnp.float32), leaf_z.astype(jnp.float32),
                        precision=lax.Precision.HIGHEST)
    leaf_split = leaf_u.reshape(4, COUPLE_BLOCKS, BLOCK_ROWS, source_count)
    parent_values = leaf_split[:, :half_count].reshape(-1, BLOCK_ROWS, source_count)
    parent_nodes = jnp.repeat(parents, half_count).astype(jnp.int32)
    parent_blocks = blocks_leaf[:, :half_count].reshape(-1).astype(jnp.int32)
    branch_update = place_blocks(parent_values, parent_nodes, parent_blocks, branch_blocks, 2)
    branch_y = (load_branch.astype(jnp.float32) - branch_update).astype(jnp.bfloat16)
    field_branch = solve_level(inverse_branch, branch_y)
    branch_z = field_branch.astype(jnp.bfloat16)
    branch_u = jnp.einsum("nrw,nwc->nrc", coupling_branch.astype(jnp.float32), branch_z.astype(jnp.float32),
                          precision=lax.Precision.HIGHEST)
    upper_values = leaf_split[:, half_count:].reshape(-1, BLOCK_ROWS, source_count)
    upper_blocks = (blocks_leaf[:, half_count:] - branch_blocks).reshape(-1).astype(jnp.int32)
    upper_nodes = jnp.zeros(upper_blocks.shape, jnp.int32)
    branch_values = branch_u.reshape(-1, BLOCK_ROWS, source_count)
    branch_targets = blocks_branch.reshape(-1).astype(jnp.int32)
    branch_nodes = jnp.zeros(branch_targets.shape, jnp.int32)
    root_update = place_blocks(upper_values, upper_nodes, upper_blocks, root_blocks, 1)[0]
    root_update = root_update + place_blocks(branch_values, branch_nodes, branch_targets, root_blocks, 1)[0]
    root_y = (load_root.astype(jnp.float32) - root_update).astype(jnp.bfloat16)
    field_root = jnp.dot(inverse_root, root_y, preferred_element_type=jnp.float32)
    coverage_root = jnp.sum(field_root * field_root, axis=-1)
    coverage_branch = jnp.sum(field_branch * field_branch, axis=-1)
    coverage_leaf = jnp.sum(field_leaf * field_leaf, axis=-1)
    return field_root, field_branch, field_leaf, coverage_root, coverage_branch, coverage_leaf
```

```python
import jax
import jax.numpy as jnp
from jax import lax
from jax.experimental import pallas as pl
from jax.experimental.pallas import tpu as pltpu
from jax.sharding import PartitionSpec as P

MESH = pl.DeviceIdType.MESH
F32 = jnp.float32
BF16 = jnp.bfloat16
OFFSETS = (0, -1, 1, 2)


class Place:
    def __init__(self):
        self.me = lax.axis_index("row")
        chip = self.me // 2
        self.core = lax.rem(self.me, 2)
        self.chip = chip
        self.x = chip // 4
        self.z = lax.rem(chip, 4)

    def row(self, dx, dz):
        x = lax.rem(self.x + (dx + 4), 4)
        z = lax.rem(self.z + (dz + 4), 4)
        return (x * 4 + z) * 2 + self.core

    def along(self, axis, d):
        return self.row(d, 0) if axis == "x" else self.row(0, d)

    def partner(self):
        return self.me + 1 - 2 * self.core

    def entry(self, extra=()):
        barrier = pltpu.get_barrier_semaphore()
        peers = [{"row": r} for r in (self.row(1, 0), self.row(-1, 0), self.row(0, 1), self.row(0, -1), self.partner())]
        peers += list(extra)
        for peer in peers:
            pl.semaphore_signal(barrier, inc=1, device_id=peer, device_id_type=MESH)
        pl.semaphore_wait(barrier, len(peers))


def push(src, dst, send, recv, row):
    pltpu.make_async_remote_copy(
        src_ref=src, dst_ref=dst, send_sem=send, recv_sem=recv, device_id={"row": row}, device_id_type=MESH
    ).start()


def await_bytes(ref, sem):
    pltpu.make_async_copy(ref, ref, sem).wait()


def gather(place, buf, own, send, recv, pair):
    axes = (("x", "z"), ("z", "x"))

    def owner(g, o1, o2):
        return place.row(o1, o2) if g == 0 else place.row(o2, o1)

    def piece(g, o1, o2, q0, q1):
        dst = buf.at[owner(g, o1, o2), 2 * g + q0 : 2 * g + q1]
        if (o1, o2) == (0, 0):
            return own.at[2 * g + q0 : 2 * g + q1], dst
        return dst, dst

    def slot(g, phase, o1, k):
        ring = 0 if phase == 1 else 1 + OFFSETS.index(o1)
        return recv.at[(g * 5 + ring) * 3 + k]

    def ring_send(g, phase, o1):
        src, dst = piece(g, o1, 0, 0, 2)
        for d, k in ((1, 0), (-1, 1)):
            push(src, dst, send, slot(g, phase, o1, k), place.along(axes[g][phase - 1], d))

    def to_partner(g, o1, o2):
        src, dst = piece(g, o1, o2, 0, 2)
        push(src, dst, send, pair, place.partner())

    def arrived(g, phase, o1, side):
        at = (side, 0) if phase == 1 else (o1, side)
        _, whole = piece(g, at[0], at[1], 0, 2)
        k = 0 if side == -1 else 1
        await_bytes(whole, slot(g, phase, o1, k))
        _, part = piece(g, at[0], at[1], k, k + 1)
        push(part, part, send, slot(g, phase, o1, 2), place.along(axes[g][phase - 1], -side))
        if phase == 1:
            ring_send(g, 2, side)
        to_partner(g, *at)

    def far(g, phase, o1):
        at = (2, 0) if phase == 1 else (o1, 2)
        _, whole = piece(g, at[0], at[1], 0, 2)
        await_bytes(whole, slot(g, phase, o1, 2))
        if phase == 1:
            ring_send(g, 2, 2)
        to_partner(g, *at)

    for g in (0, 1):
        ring_send(g, 1, 0)
    for g in (0, 1):
        ring_send(g, 2, 0)
        to_partner(g, 0, 0)
    yield
    events = []
    for side in (-1, 1):
        events += [(arrived, g, 1, 0, side) for g in (0, 1)]
    for side in (-1, 1):
        events += [(arrived, g, 2, 0, side) for g in (0, 1)]
    events += [(far, g, 1, 0) for g in (0, 1)]
    for o1 in (-1, 1):
        for side in (-1, 1):
            events += [(arrived, g, 2, o1, side) for g in (0, 1)]
    events += [(far, g, 2, 0) for g in (0, 1)]
    for side in (-1, 1):
        events += [(arrived, g, 2, 2, side) for g in (0, 1)]
    for o1 in (-1, 1, 2):
        events += [(far, g, 2, o1) for g in (0, 1)]
    for event in events:
        event[0](*event[1:])
        yield
    await_bytes(buf.at[0:16], pair)
    await_bytes(buf.at[0:31], send)
    yield


def reduce(place, s, t1, t2, t3, t4, out, send, recv):
    axes = (("x", "z"), ("z", "x"))

    def coord(axis, d):
        return lax.rem((place.x if axis == "x" else place.z) + (d + 4), 4)

    def line(g, d, q):
        a = coord(axes[g][0], d)
        return (a, slice(None), q) if g == 0 else (slice(None), a, q)

    def cell(g, d, q):
        a = coord(axes[g][0], 0)
        b = coord(axes[g][1], d)
        return (a, b, q) if g == 0 else (b, a, q)

    def both(g):
        return slice(2 * g, 2 * g + 2)

    def slot(g, k):
        return recv.at[g * 8 + k]

    for phase, index, ta, tb in ((0, line, t1, t2), (1, cell, t3, t4)):
        for g in (0, 1):
            axis = axes[g][phase]
            for k, d in ((0, -1), (1, 1)):
                push(s.at[index(g, 2 * d, 2 * g + k)], ta.at[g, k], send, slot(g, 4 * phase + k), place.along(axis, d))
        yield
        for g in (0, 1):
            axis = axes[g][phase]
            for k, d in ((0, -1), (1, 1)):
                await_bytes(ta.at[g, k], slot(g, 4 * phase + k))
                at = index(g, d, 2 * g + k)
                s[at] = (s[at].astype(F32) + ta[g, k].astype(F32)).astype(BF16)
                push(s.at[index(g, d, both(g))], tb.at[g, k], send, slot(g, 4 * phase + 2 + k), place.along(axis, d))
            yield
        for g in (0, 1):
            for k in (0, 1):
                await_bytes(tb.at[g, k], slot(g, 4 * phase + 2 + k))
            at = index(g, 0, both(g))
            total = s[at].astype(F32) + tb[g, 0].astype(F32) + tb[g, 1].astype(F32)
            if phase == 0:
                s[at] = total.astype(BF16)
            else:
                out[both(g)] = total.astype(BF16)
            yield


def couple(place, c_ref, z_ref, p_send, q_recv, s, send, recv, rows, per_node, pieces):
    step = 16 // pieces

    def product(owner):
        node = owner // per_node
        first = pl.multiple_of(lax.rem(owner, per_node) * rows, rows)
        return jnp.dot(c_ref[node, pl.ds(first, rows), :], z_ref[node], preferred_element_type=F32)

    shape = p_send.shape[1:]
    for piece in range(pieces):

        @pl.loop(piece * step, piece * step + step)
        def _(chip):
            p_send[chip] = product(chip * 2 + 1 - place.core).astype(BF16).reshape(shape)
            push(p_send.at[chip], q_recv.at[chip], send, recv.at[chip], place.partner())

        yield
    for piece in range(pieces):

        @pl.loop(piece * step, piece * step + step)
        def _(chip):
            await_bytes(q_recv.at[chip], recv.at[chip])
            other = q_recv[chip].reshape(rows, shape[2]).astype(F32)
            s[chip // 4, lax.rem(chip, 4)] = (product(chip * 2 + place.core) + other).astype(BF16).reshape(shape)

        yield


def drain(*tasks):
    for task in tasks:
        for _ in task:
            pass


def advance(task, count):
    for _ in range(count):
        if next(task, 0) == 0:
            return


def leaf_kernel(
    load_leaf, load_branch, load_root, inverse, coupling,
    field, b_branch, b_root, u_all,
    b, a, c, z, p_send, q_recv, s, t1, t2, t3, t4, u_own,
    send, recv_l, recv_b, recv_r, recv_u, pair, recv_s, recv_q, local,
):
    place = Place()
    me = place.me
    copies = [
        pltpu.make_async_copy(inverse, a, local.at[0]),
        pltpu.make_async_copy(coupling, c, local.at[1]),
        pltpu.make_async_copy(load_leaf, b.at[me], local.at[2]),
        pltpu.make_async_copy(load_branch, b_branch.at[me], local.at[3]),
        pltpu.make_async_copy(load_root, b_root.at[me], local.at[4]),
    ]
    for copy in copies:
        copy.start()
    place.entry()
    ag_leaf = gather(place, b, load_leaf, send.at[0], recv_l, pair.at[0])
    ag_branch = gather(place, b_branch, load_branch, send.at[1], recv_b, pair.at[1])
    ag_root = gather(place, b_root, load_root, send.at[2], recv_r, pair.at[2])
    ag_u = gather(place, u_all, u_own, send.at[3], recv_u, pair.at[3])
    advance(ag_leaf, 27)
    advance(ag_branch, 1)
    for copy in copies[:3]:
        copy.wait()
    drain(ag_leaf)

    def leaf():
        for n in range(4):
            field[n] = jnp.zeros_like(field.at[n])

            @pl.loop(0, place.chip // 4 + 1)
            def _(j):
                cols = pl.ds(pl.multiple_of(j * 1024, 1024), 1024)
                rows = b[pl.ds(j * 8, 8), n].reshape(1024, b.shape[3])
                field[n] += jnp.dot(a[n, :, cols], rows, preferred_element_type=F32)

            z[n] = field[n].astype(BF16)
            yield
        yield from couple(place, c, z, p_send, q_recv, s, send.at[4], recv_q, 256, 8, 4)

    for _ in leaf():
        advance(ag_branch, 1)
    rs = reduce(place, s, t1, t2, t3, t4, u_own, send.at[4], recv_s)
    for _ in rs:
        advance(ag_branch, 2)
    mine = pltpu.make_async_copy(u_own, u_all.at[me], local.at[5])
    mine.start()
    advance(ag_u, 1)
    drain(ag_branch)
    advance(ag_root, 1)
    for _ in ag_u:
        advance(ag_root, 1)
    drain(ag_root)
    await_bytes(u_all.at[0:31], send.at[4])
    mine.wait()
    for copy in copies[3:]:
        copy.wait()


def correct(out, index, a_cols, ids, u_rows, ag):
    for k in range(8):
        ag[:, k * 128 : k * 128 + 128] = a_cols(pl.multiple_of(ids(k) * 128, 128))
    out[index] -= jnp.dot(ag[...], u_rows.reshape(1024, u_rows.shape[-1]), preferred_element_type=F32)


def branch_kernel(
    blocks_leaf, parents, a_branch, b_branch, u_all,
    field, z,
    ab, bb, ul, ag, sems,
):
    width = bb.shape[3]
    copies = []
    for j in range(8):
        cols = slice(1024 * j, 1024 * j + 1024)
        copies.append(pltpu.make_async_copy(b_branch.at[4 * j : 4 * j + 4], bb.at[4 * j : 4 * j + 4], sems.at[2 * j]))
        copies.append(pltpu.make_async_copy(a_branch.at[:, :, cols], ab.at[:, :, cols], sems.at[2 * j + 1]))
    for i in range(4):
        copies.append(pltpu.make_async_copy(u_all.at[8 * i : 8 * i + 4], ul.at[i], sems.at[16 + i]))
    for copy in copies:
        copy.start()
    trips = lax.axis_index("row") // 4 + 1
    field[...] = jnp.zeros_like(field)
    for j in range(8):
        copies[2 * j].wait()
        copies[2 * j + 1].wait()

        @pl.when(j < trips)
        def _():
            for n in range(2):
                rows = bb[4 * j : 4 * j + 4, 2 * n : 2 * n + 2].reshape(1024, width)
                field[n] += jnp.dot(ab[n, :, 1024 * j : 1024 * j + 1024], rows, preferred_element_type=F32)

    for copy in copies[16:]:
        copy.wait()

    @pl.loop(0, 4)
    def _(i):
        n = parents[i]
        correct(field, n, lambda col: ab[n, :, pl.ds(col, 128)], lambda k: blocks_leaf[i, k], ul[i], ag)

    z[...] = field[...].astype(BF16)


def upper_kernel(
    z_in, c_branch, a_root, b_root,
    field_root, u2,
    zb, cb, ar, br, p_send, q_recv, s, t1, t2, t3, t4, u_own,
    send, recv_u, pair, recv_s, recv_q, local,
):
    place = Place()
    me = place.me
    width = br.shape[3]
    pairs = ((z_in, zb), (c_branch, cb), (b_root, br), (a_root, ar))
    copies = [pltpu.make_async_copy(src, dst, local.at[k]) for k, (src, dst) in enumerate(pairs)]
    for copy in copies:
        copy.start()
    place.entry()
    copies[0].wait()
    copies[1].wait()
    drain(couple(place, cb, zb, p_send, q_recv, s, send.at[0], recv_q, 128, 16, 1))

    def root():
        trips = me // 4 + 1
        copies[2].wait()
        copies[3].wait()
        field_root[...] = jnp.zeros_like(field_root)
        for h in range(4):

            @pl.loop(jnp.minimum(trips, 2 * h), jnp.minimum(trips, 2 * h + 2))
            def _(j):
                cols = pl.ds(pl.multiple_of(j * 1024, 1024), 1024)
                rows = br[pl.ds(j * 4, 4)].reshape(1024, width)
                field_root[...] += jnp.dot(ar[:, cols], rows, preferred_element_type=F32)

            yield

    work = root()
    rs = reduce(place, s, t1, t2, t3, t4, u_own, send.at[0], recv_s)
    for _ in rs:
        advance(work, 1)
    drain(work)
    mine = pltpu.make_async_copy(u_own, u2.at[me], local.at[4])
    mine.start()
    drain(gather(place, u2, u_own, send.at[1], recv_u, pair.at[0]))
    await_bytes(u2.at[0:31], send.at[0])
    mine.wait()


def root_kernel(
    blocks_branch, blocks_leaf, a_root, u_all, u2_in, partial,
    field,
    ar, ul, ub, ag, sems,
):
    copies = [pltpu.make_async_copy(a_root, ar, sems.at[0]), pltpu.make_async_copy(u2_in, ub, sems.at[1])]
    for i in range(4):
        copies.append(pltpu.make_async_copy(u_all.at[8 * i + 4 : 8 * i + 8], ul.at[i], sems.at[2 + i]))
    for copy in copies:
        copy.start()
    field[...] = partial[...]
    for copy in copies:
        copy.wait()

    @pl.loop(0, 4)
    def _(i):
        correct(field, ..., lambda col: ar[:, pl.ds(col, 128)], lambda k: blocks_leaf[i, 8 + k] - 64, ul[i], ag)

    @pl.loop(0, 4)
    def _(i):
        p, h = i // 2, lax.rem(i, 2)
        rows = ub[pl.ds(i * 8, 8)]
        correct(field, ..., lambda col: ar[:, pl.ds(col, 128)], lambda k: blocks_branch[p, 8 * h + k], rows, ag)


def reduce_scratch(q, c):
    return [
        pltpu.VMEM((16, 4, q, c), BF16),
        pltpu.VMEM((16, 4, q, c), BF16),
        pltpu.VMEM((4, 4, 4, q, c), BF16),
        pltpu.VMEM((2, 2, 4, q, c), BF16),
        pltpu.VMEM((2, 2, 4, 2, q, c), BF16),
        pltpu.VMEM((2, 2, q, c), BF16),
        pltpu.VMEM((2, 2, 2, q, c), BF16),
        pltpu.VMEM((4, q, c), BF16),
    ]


def local(
    load_root, load_branch, load_leaf, inverse_root, inverse_branch, inverse_leaf,
    coupling_branch, coupling_leaf, blocks_branch, blocks_leaf, parents,
):
    c = load_leaf.shape[2]
    dma = pltpu.SemaphoreType.DMA
    anywhere = pl.BlockSpec(memory_space=pl.ANY)
    vmem = pl.BlockSpec(memory_space=pltpu.VMEM)
    smem = pl.BlockSpec(memory_space=pltpu.SMEM)
    field_leaf, b_branch, b_root, u_all = pl.pallas_call(
        leaf_kernel,
        out_shape=(
            jax.ShapeDtypeStruct((4, 128, c), F32),
            jax.ShapeDtypeStruct((32, 4, 128, c), BF16),
            jax.ShapeDtypeStruct((32, 4, 64, c), BF16),
            jax.ShapeDtypeStruct((32, 4, 64, c), BF16),
        ),
        in_specs=[anywhere] * 5,
        out_specs=(vmem, anywhere, anywhere, anywhere),
        scratch_shapes=[
            pltpu.VMEM((32, 4, 128, c), BF16),
            pltpu.VMEM((4, 128, 4096), BF16),
            pltpu.VMEM((4, 2048, 128), BF16),
            pltpu.VMEM((4, 128, c), BF16),
            *reduce_scratch(64, c),
            dma((5,)), dma((30,)), dma((30,)), dma((30,)), dma((30,)), dma((4,)), dma((16,)), dma((16,)), dma((6,)),
        ],
        compiler_params=pltpu.CompilerParams(
            collective_id=0, has_side_effects=True, vmem_limit_bytes=60 * 1024 * 1024
        ),
        name="leaf_level",
    )(load_leaf, load_branch.reshape(4, 128, c), load_root.reshape(4, 64, c), inverse_leaf, coupling_leaf)
    field_branch, z_branch = pl.pallas_call(
        branch_kernel,
        out_shape=(jax.ShapeDtypeStruct((2, 256, c), F32), jax.ShapeDtypeStruct((2, 256, c), BF16)),
        in_specs=[smem] * 2 + [anywhere] * 3,
        out_specs=(vmem, vmem),
        scratch_shapes=[
            pltpu.VMEM((2, 256, 8192), BF16),
            pltpu.VMEM((32, 4, 128, c), BF16),
            pltpu.VMEM((4, 4, 4, 64, c), BF16),
            pltpu.VMEM((256, 1024), BF16),
            dma((20,)),
        ],
        compiler_params=pltpu.CompilerParams(vmem_limit_bytes=60 * 1024 * 1024),
        name="branch_level",
    )(blocks_leaf, parents, inverse_branch, b_branch, u_all)
    partial_root, u2 = pl.pallas_call(
        upper_kernel,
        out_shape=(jax.ShapeDtypeStruct((256, c), F32), jax.ShapeDtypeStruct((32, 4, 32, c), BF16)),
        in_specs=[anywhere] * 4,
        out_specs=(vmem, anywhere),
        scratch_shapes=[
            pltpu.VMEM((2, 256, c), BF16),
            pltpu.VMEM((2, 2048, 256), BF16),
            pltpu.VMEM((256, 8192), BF16),
            pltpu.VMEM((32, 4, 64, c), BF16),
            *reduce_scratch(32, c),
            dma((2,)), dma((30,)), dma((1,)), dma((16,)), dma((16,)), dma((5,)),
        ],
        compiler_params=pltpu.CompilerParams(
            collective_id=1, has_side_effects=True, vmem_limit_bytes=60 * 1024 * 1024
        ),
        name="branch_updates",
    )(z_branch, coupling_branch, inverse_root, b_root)
    field_root = pl.pallas_call(
        root_kernel,
        out_shape=jax.ShapeDtypeStruct((256, c), F32),
        in_specs=[smem] * 2 + [anywhere] * 3 + [vmem],
        out_specs=vmem,
        scratch_shapes=[
            pltpu.VMEM((256, 8192), BF16),
            pltpu.VMEM((4, 4, 4, 64, c), BF16),
            pltpu.VMEM((32, 4, 32, c), BF16),
            pltpu.VMEM((256, 1024), BF16),
            dma((6,)),
        ],
        compiler_params=pltpu.CompilerParams(vmem_limit_bytes=60 * 1024 * 1024),
        name="root_level",
    )(blocks_branch, blocks_leaf, inverse_root, u_all, u2, partial_root)
    coverage_root, coverage_branch, coverage_leaf = lax.psum(
        (
            jnp.sum(field_root * field_root, axis=-1),
            jnp.sum(field_branch * field_branch, axis=-1),
            jnp.sum(field_leaf * field_leaf, axis=-1),
        ),
        "src",
    )
    return (field_root, field_branch, field_leaf, coverage_root, coverage_branch, coverage_leaf)


def solution(mesh):
    return jax.shard_map(
        local,
        mesh=mesh,
        in_specs=(
            P("row", "src"),
            P(None, "row", "src"),
            P(None, "row", "src"),
            P("row", None),
            P(None, "row", None),
            P(None, "row", None),
            P(None, None, "row"),
            P(None, None, "row"),
            P(),
            P(),
            P(),
        ),
        out_specs=(
            P("row", "src"),
            P(None, "row", "src"),
            P(None, "row", "src"),
            P("row"),
            P(None, "row"),
            P(None, "row"),
        ),
        check_vma=False,
    )
```

```python
import jax
import jax.numpy as jnp
from jax import lax
from jax.experimental import pallas as pl
from jax.experimental.pallas import tpu as pltpu
from jax.sharding import PartitionSpec as P

MESH = pl.DeviceIdType.MESH
F32 = jnp.float32
BF16 = jnp.bfloat16
OFFSETS = (0, -1, 1, 2)


class Place:
    def __init__(self):
        self.me = lax.axis_index("row")
        chip = self.me // 2
        self.core = lax.rem(self.me, 2)
        self.chip = chip
        self.x = chip // 4
        self.z = lax.rem(chip, 4)

    def row(self, dx, dz):
        x = lax.rem(self.x + (dx + 4), 4)
        z = lax.rem(self.z + (dz + 4), 4)
        return (x * 4 + z) * 2 + self.core

    def along(self, axis, d):
        return self.row(d, 0) if axis == "x" else self.row(0, d)

    def partner(self):
        return self.me + 1 - 2 * self.core

    def entry(self, extra=()):
        barrier = pltpu.get_barrier_semaphore()
        peers = [{"row": r} for r in (self.row(1, 0), self.row(-1, 0), self.row(0, 1), self.row(0, -1), self.partner())]
        peers += list(extra)
        for peer in peers:
            pl.semaphore_signal(barrier, inc=1, device_id=peer, device_id_type=MESH)
        pl.semaphore_wait(barrier, len(peers))


def push(src, dst, send, recv, row):
    pltpu.make_async_remote_copy(
        src_ref=src, dst_ref=dst, send_sem=send, recv_sem=recv, device_id={"row": row}, device_id_type=MESH
    ).start()


def await_bytes(ref, sem):
    pltpu.make_async_copy(ref, ref, sem).wait()


def gather(place, buf, own, send, recv, pair):
    axes = (("x", "z"), ("z", "x"))

    def owner(g, o1, o2):
        return place.row(o1, o2) if g == 0 else place.row(o2, o1)

    def piece(g, o1, o2, q0, q1):
        dst = buf.at[owner(g, o1, o2), 2 * g + q0 : 2 * g + q1]
        if (o1, o2) == (0, 0):
            return own.at[2 * g + q0 : 2 * g + q1], dst
        return dst, dst

    def slot(g, phase, o1, k):
        ring = 0 if phase == 1 else 1 + OFFSETS.index(o1)
        return recv.at[(g * 5 + ring) * 3 + k]

    def ring_send(g, phase, o1):
        src, dst = piece(g, o1, 0, 0, 2)
        for d, k in ((1, 0), (-1, 1)):
            push(src, dst, send, slot(g, phase, o1, k), place.along(axes[g][phase - 1], d))

    def to_partner(g, o1, o2):
        src, dst = piece(g, o1, o2, 0, 2)
        push(src, dst, send, pair, place.partner())

    def arrived(g, phase, o1, side):
        at = (side, 0) if phase == 1 else (o1, side)
        _, whole = piece(g, at[0], at[1], 0, 2)
        k = 0 if side == -1 else 1
        await_bytes(whole, slot(g, phase, o1, k))
        _, part = piece(g, at[0], at[1], k, k + 1)
        push(part, part, send, slot(g, phase, o1, 2), place.along(axes[g][phase - 1], -side))
        if phase == 1:
            ring_send(g, 2, side)
        to_partner(g, *at)

    def far(g, phase, o1):
        at = (2, 0) if phase == 1 else (o1, 2)
        _, whole = piece(g, at[0], at[1], 0, 2)
        await_bytes(whole, slot(g, phase, o1, 2))
        if phase == 1:
            ring_send(g, 2, 2)
        to_partner(g, *at)

    for g in (0, 1):
        ring_send(g, 1, 0)
    for g in (0, 1):
        ring_send(g, 2, 0)
        to_partner(g, 0, 0)
    yield
    events = []
    for side in (-1, 1):
        events += [(arrived, g, 1, 0, side) for g in (0, 1)]
    for side in (-1, 1):
        events += [(arrived, g, 2, 0, side) for g in (0, 1)]
    events += [(far, g, 1, 0) for g in (0, 1)]
    for o1 in (-1, 1):
        for side in (-1, 1):
            events += [(arrived, g, 2, o1, side) for g in (0, 1)]
    events += [(far, g, 2, 0) for g in (0, 1)]
    for side in (-1, 1):
        events += [(arrived, g, 2, 2, side) for g in (0, 1)]
    for o1 in (-1, 1, 2):
        events += [(far, g, 2, o1) for g in (0, 1)]
    for event in events:
        event[0](*event[1:])
        yield
    await_bytes(buf.at[0:16], pair)
    await_bytes(buf.at[0:31], send)
    yield


def reduce(place, s, t1, t2, t3, t4, out, send, recv):
    axes = (("x", "z"), ("z", "x"))

    def coord(axis, d):
        return lax.rem((place.x if axis == "x" else place.z) + (d + 4), 4)

    def line(g, d, q):
        a = coord(axes[g][0], d)
        return (a, slice(None), q) if g == 0 else (slice(None), a, q)

    def cell(g, d, q):
        a = coord(axes[g][0], 0)
        b = coord(axes[g][1], d)
        return (a, b, q) if g == 0 else (b, a, q)

    def both(g):
        return slice(2 * g, 2 * g + 2)

    def slot(g, k):
        return recv.at[g * 8 + k]

    for phase, index, ta, tb in ((0, line, t1, t2), (1, cell, t3, t4)):
        for g in (0, 1):
            axis = axes[g][phase]
            for k, d in ((0, -1), (1, 1)):
                push(s.at[index(g, 2 * d, 2 * g + k)], ta.at[g, k], send, slot(g, 4 * phase + k), place.along(axis, d))
        yield
        for g in (0, 1):
            axis = axes[g][phase]
            for k, d in ((0, -1), (1, 1)):
                await_bytes(ta.at[g, k], slot(g, 4 * phase + k))
                at = index(g, d, 2 * g + k)
                s[at] = (s[at].astype(F32) + ta[g, k].astype(F32)).astype(BF16)
                push(s.at[index(g, d, both(g))], tb.at[g, k], send, slot(g, 4 * phase + 2 + k), place.along(axis, d))
            yield
        for g in (0, 1):
            for k in (0, 1):
                await_bytes(tb.at[g, k], slot(g, 4 * phase + 2 + k))
            at = index(g, 0, both(g))
            total = s[at].astype(F32) + tb[g, 0].astype(F32) + tb[g, 1].astype(F32)
            if phase == 0:
                s[at] = total.astype(BF16)
            else:
                out[both(g)] = total.astype(BF16)
            yield


def couple(place, c_ref, z_ref, p_send, q_recv, s, send, recv, rows, per_node, pieces):
    step = 16 // pieces

    def product(owner):
        node = owner // per_node
        first = pl.multiple_of(lax.rem(owner, per_node) * rows, rows)
        return jnp.dot(c_ref[node, pl.ds(first, rows), :], z_ref[node], preferred_element_type=F32)

    shape = p_send.shape[1:]
    for piece in range(pieces):

        @pl.loop(piece * step, piece * step + step)
        def _(chip):
            p_send[chip] = product(chip * 2 + 1 - place.core).astype(BF16).reshape(shape)
            push(p_send.at[chip], q_recv.at[chip], send, recv.at[chip], place.partner())

        yield
    for piece in range(pieces):

        @pl.loop(piece * step, piece * step + step)
        def _(chip):
            await_bytes(q_recv.at[chip], recv.at[chip])
            other = q_recv[chip].reshape(rows, shape[2]).astype(F32)
            s[chip // 4, lax.rem(chip, 4)] = (product(chip * 2 + place.core) + other).astype(BF16).reshape(shape)

        yield


def drain(*tasks):
    for task in tasks:
        for _ in task:
            pass


def advance(task, count):
    for _ in range(count):
        if next(task, 0) == 0:
            return


def leaf_kernel(
    load_leaf, load_branch, inverse, coupling, a_branch,
    field, field_branch, u_all,
    b, bb, a, ab, c, z, p_send, q_recv, s, t1, t2, t3, t4, u_own,
    send, recv_l, recv_b, recv_u, pair, recv_s, recv_q, local,
):
    place = Place()
    me = place.me
    width = b.shape[3]
    copies = [
        pltpu.make_async_copy(inverse, a, local.at[0]),
        pltpu.make_async_copy(coupling, c, local.at[1]),
        pltpu.make_async_copy(load_leaf, b.at[me], local.at[2]),
        pltpu.make_async_copy(load_branch, bb.at[me], local.at[3]),
        pltpu.make_async_copy(a_branch, ab, local.at[4]),
    ]
    for copy in copies:
        copy.start()
    place.entry()
    ag_leaf = gather(place, b, load_leaf, send.at[0], recv_l, pair.at[0])
    ag_branch = gather(place, bb, load_branch, send.at[1], recv_b, pair.at[1])
    ag_u = gather(place, u_all, u_own, send.at[2], recv_u, pair.at[2])
    advance(ag_leaf, 27)
    advance(ag_branch, 1)
    for copy in copies[:3]:
        copy.wait()
    drain(ag_leaf)

    def leaf():
        for n in range(4):
            field[n] = jnp.zeros_like(field.at[n])

            @pl.loop(0, place.chip // 4 + 1)
            def _(j):
                cols = pl.ds(pl.multiple_of(j * 1024, 1024), 1024)
                rows = b[pl.ds(j * 8, 8), n].reshape(1024, width)
                field[n] += jnp.dot(a[n, :, cols], rows, preferred_element_type=F32)

            z[n] = field[n].astype(BF16)
            yield
        yield from couple(place, c, z, p_send, q_recv, s, send.at[3], recv_q, 256, 8, 4)

    def branch():
        trips = me // 4 + 1
        copies[3].wait()
        copies[4].wait()
        field_branch[...] = jnp.zeros_like(field_branch)
        for h in range(4):
            for n in range(2):

                @pl.loop(jnp.minimum(trips, 2 * h), jnp.minimum(trips, 2 * h + 2))
                def _(j):
                    cols = pl.ds(pl.multiple_of(j * 1024, 1024), 1024)
                    rows = bb[pl.ds(j * 4, 4), 2 * n : 2 * n + 2].reshape(1024, width)
                    field_branch[n] += jnp.dot(ab[n, :, cols], rows, preferred_element_type=F32)

                yield

    for _ in leaf():
        advance(ag_branch, 1)
    rs = reduce(place, s, t1, t2, t3, t4, u_own, send.at[3], recv_s)
    for _ in rs:
        advance(ag_branch, 2)
    mine = pltpu.make_async_copy(u_own, u_all.at[me], local.at[5])
    mine.start()
    advance(ag_u, 1)
    drain(ag_branch)
    work = branch()
    for _ in ag_u:
        advance(work, 1)
    drain(work)
    await_bytes(u_all.at[0:31], send.at[3])
    mine.wait()


def correct(out, index, a_cols, ids, u_rows, ag):
    for k in range(8):
        ag[:, k * 128 : k * 128 + 128] = a_cols(pl.multiple_of(ids(k) * 128, 128))
    out[index] -= jnp.dot(ag[...], u_rows.reshape(1024, u_rows.shape[-1]), preferred_element_type=F32)


def branch_kernel(
    blocks_leaf, parents, a_branch, u_all, partial,
    field, z,
    ab, ul, ag, sems,
):
    copies = [pltpu.make_async_copy(a_branch, ab, sems.at[4])]
    for i in range(4):
        copies.append(pltpu.make_async_copy(u_all.at[8 * i : 8 * i + 4], ul.at[i], sems.at[i]))
    for copy in copies:
        copy.start()
    field[...] = partial[...]
    for copy in copies:
        copy.wait()

    @pl.loop(0, 4)
    def _(i):
        n = parents[i]
        correct(field, n, lambda col: ab[n, :, pl.ds(col, 128)], lambda k: blocks_leaf[i, k], ul[i], ag)

    z[...] = field[...].astype(BF16)


def upper_kernel(
    z_in, c_branch, a_root, load_root,
    field_root, u2,
    zb, cb, ar, br, p_send, q_recv, s, t1, t2, t3, t4, u_own,
    send, recv_r, recv_u, pair, recv_s, recv_q, local,
):
    place = Place()
    me = place.me
    width = br.shape[3]
    pairs = ((z_in, zb), (c_branch, cb), (load_root, br.at[me]), (a_root, ar))
    copies = [pltpu.make_async_copy(src, dst, local.at[k]) for k, (src, dst) in enumerate(pairs)]
    for copy in copies:
        copy.start()
    place.entry()
    ag_root = gather(place, br, load_root, send.at[2], recv_r, pair.at[1])
    advance(ag_root, 1)
    copies[0].wait()
    copies[1].wait()
    for _ in couple(place, cb, zb, p_send, q_recv, s, send.at[0], recv_q, 128, 16, 4):
        advance(ag_root, 1)

    def root():
        trips = me // 4 + 1
        copies[2].wait()
        copies[3].wait()
        field_root[...] = jnp.zeros_like(field_root)
        for h in range(4):

            @pl.loop(jnp.minimum(trips, 2 * h), jnp.minimum(trips, 2 * h + 2))
            def _(j):
                cols = pl.ds(pl.multiple_of(j * 1024, 1024), 1024)
                rows = br[pl.ds(j * 4, 4)].reshape(1024, width)
                field_root[...] += jnp.dot(ar[:, cols], rows, preferred_element_type=F32)

            yield

    rs = reduce(place, s, t1, t2, t3, t4, u_own, send.at[0], recv_s)
    for _ in rs:
        advance(ag_root, 2)
    mine = pltpu.make_async_copy(u_own, u2.at[me], local.at[4])
    mine.start()
    ag_u = gather(place, u2, u_own, send.at[1], recv_u, pair.at[0])
    advance(ag_u, 1)
    drain(ag_root)
    work = root()
    for _ in ag_u:
        advance(work, 1)
    drain(work)
    await_bytes(u2.at[0:31], send.at[0])
    mine.wait()


def root_kernel(
    blocks_branch, blocks_leaf, a_root, u_all, u2_in, partial,
    field,
    ar, ul, ub, ag, sems,
):
    copies = [pltpu.make_async_copy(a_root, ar, sems.at[0]), pltpu.make_async_copy(u2_in, ub, sems.at[1])]
    for i in range(4):
        copies.append(pltpu.make_async_copy(u_all.at[8 * i + 4 : 8 * i + 8], ul.at[i], sems.at[2 + i]))
    for copy in copies:
        copy.start()
    field[...] = partial[...]
    for copy in copies:
        copy.wait()

    @pl.loop(0, 4)
    def _(i):
        correct(field, ..., lambda col: ar[:, pl.ds(col, 128)], lambda k: blocks_leaf[i, 8 + k] - 64, ul[i], ag)

    @pl.loop(0, 4)
    def _(i):
        p, h = i // 2, lax.rem(i, 2)
        rows = ub[pl.ds(i * 8, 8)]
        correct(field, ..., lambda col: ar[:, pl.ds(col, 128)], lambda k: blocks_branch[p, 8 * h + k], rows, ag)


def reduce_scratch(q, c):
    return [
        pltpu.VMEM((16, 4, q, c), BF16),
        pltpu.VMEM((16, 4, q, c), BF16),
        pltpu.VMEM((4, 4, 4, q, c), BF16),
        pltpu.VMEM((2, 2, 4, q, c), BF16),
        pltpu.VMEM((2, 2, 4, 2, q, c), BF16),
        pltpu.VMEM((2, 2, q, c), BF16),
        pltpu.VMEM((2, 2, 2, q, c), BF16),
        pltpu.VMEM((4, q, c), BF16),
    ]


def local(
    load_root, load_branch, load_leaf, inverse_root, inverse_branch, inverse_leaf,
    coupling_branch, coupling_leaf, blocks_branch, blocks_leaf, parents,
):
    c = load_leaf.shape[2]
    dma = pltpu.SemaphoreType.DMA
    anywhere = pl.BlockSpec(memory_space=pl.ANY)
    vmem = pl.BlockSpec(memory_space=pltpu.VMEM)
    smem = pl.BlockSpec(memory_space=pltpu.SMEM)
    field_leaf, partial_branch, u_all = pl.pallas_call(
        leaf_kernel,
        out_shape=(
            jax.ShapeDtypeStruct((4, 128, c), F32),
            jax.ShapeDtypeStruct((2, 256, c), F32),
            jax.ShapeDtypeStruct((32, 4, 64, c), BF16),
        ),
        in_specs=[anywhere] * 5,
        out_specs=(vmem, vmem, anywhere),
        scratch_shapes=[
            pltpu.VMEM((32, 4, 128, c), BF16),
            pltpu.VMEM((32, 4, 128, c), BF16),
            pltpu.VMEM((4, 128, 4096), BF16),
            pltpu.VMEM((2, 256, 8192), BF16),
            pltpu.VMEM((4, 2048, 128), BF16),
            pltpu.VMEM((4, 128, c), BF16),
            *reduce_scratch(64, c),
            dma((4,)), dma((30,)), dma((30,)), dma((30,)), dma((3,)), dma((16,)), dma((16,)), dma((6,)),
        ],
        compiler_params=pltpu.CompilerParams(
            collective_id=0, has_side_effects=True, vmem_limit_bytes=62 * 1024 * 1024
        ),
        name="leaf_level",
    )(load_leaf, load_branch.reshape(4, 128, c), inverse_leaf, coupling_leaf, inverse_branch)
    field_branch, z_branch = pl.pallas_call(
        branch_kernel,
        out_shape=(jax.ShapeDtypeStruct((2, 256, c), F32), jax.ShapeDtypeStruct((2, 256, c), BF16)),
        in_specs=[smem] * 2 + [anywhere] * 2 + [vmem],
        out_specs=(vmem, vmem),
        scratch_shapes=[
            pltpu.VMEM((2, 256, 8192), BF16),
            pltpu.VMEM((4, 4, 4, 64, c), BF16),
            pltpu.VMEM((256, 1024), BF16),
            dma((5,)),
        ],
        compiler_params=pltpu.CompilerParams(vmem_limit_bytes=60 * 1024 * 1024),
        name="branch_level",
    )(blocks_leaf, parents, inverse_branch, u_all, partial_branch)
    partial_root, u2 = pl.pallas_call(
        upper_kernel,
        out_shape=(jax.ShapeDtypeStruct((256, c), F32), jax.ShapeDtypeStruct((32, 4, 32, c), BF16)),
        in_specs=[anywhere] * 4,
        out_specs=(vmem, anywhere),
        scratch_shapes=[
            pltpu.VMEM((2, 256, c), BF16),
            pltpu.VMEM((2, 2048, 256), BF16),
            pltpu.VMEM((256, 8192), BF16),
            pltpu.VMEM((32, 4, 64, c), BF16),
            *reduce_scratch(32, c),
            dma((3,)), dma((30,)), dma((30,)), dma((2,)), dma((16,)), dma((16,)), dma((5,)),
        ],
        compiler_params=pltpu.CompilerParams(
            collective_id=1, has_side_effects=True, vmem_limit_bytes=60 * 1024 * 1024
        ),
        name="branch_updates",
    )(z_branch, coupling_branch, inverse_root, load_root.reshape(4, 64, c))
    field_root = pl.pallas_call(
        root_kernel,
        out_shape=jax.ShapeDtypeStruct((256, c), F32),
        in_specs=[smem] * 2 + [anywhere] * 3 + [vmem],
        out_specs=vmem,
        scratch_shapes=[
            pltpu.VMEM((256, 8192), BF16),
            pltpu.VMEM((4, 4, 4, 64, c), BF16),
            pltpu.VMEM((32, 4, 32, c), BF16),
            pltpu.VMEM((256, 1024), BF16),
            dma((6,)),
        ],
        compiler_params=pltpu.CompilerParams(vmem_limit_bytes=60 * 1024 * 1024),
        name="root_level",
    )(blocks_branch, blocks_leaf, inverse_root, u_all, u2, partial_root)
    coverage_root, coverage_branch, coverage_leaf = lax.psum(
        (
            jnp.sum(field_root * field_root, axis=-1),
            jnp.sum(field_branch * field_branch, axis=-1),
            jnp.sum(field_leaf * field_leaf, axis=-1),
        ),
        "src",
    )
    return (field_root, field_branch, field_leaf, coverage_root, coverage_branch, coverage_leaf)


def solution(mesh):
    return jax.shard_map(
        local,
        mesh=mesh,
        in_specs=(
            P("row", "src"),
            P(None, "row", "src"),
            P(None, "row", "src"),
            P("row", None),
            P(None, "row", None),
            P(None, "row", None),
            P(None, None, "row"),
            P(None, None, "row"),
            P(),
            P(),
            P(),
        ),
        out_specs=(
            P("row", "src"),
            P(None, "row", "src"),
            P(None, "row", "src"),
            P("row"),
            P(None, "row"),
            P(None, "row"),
        ),
        check_vma=False,
    )
```

```python
import jax
import jax.numpy as jnp
from jax import lax
from jax.experimental import pallas as pl
from jax.experimental.pallas import tpu as pltpu
from jax.sharding import PartitionSpec as P

MESH = pl.DeviceIdType.MESH
F32 = jnp.float32
BF16 = jnp.bfloat16
OFFSETS = (0, -1, 1, 2)


class Place:
    def __init__(self):
        self.me = lax.axis_index("row")
        chip = self.me // 2
        self.core = lax.rem(self.me, 2)
        self.chip = chip
        self.x = chip // 4
        self.z = lax.rem(chip, 4)

    def row(self, dx, dz):
        x = lax.rem(self.x + (dx + 4), 4)
        z = lax.rem(self.z + (dz + 4), 4)
        return (x * 4 + z) * 2 + self.core

    def along(self, axis, d):
        return self.row(d, 0) if axis == "x" else self.row(0, d)

    def partner(self):
        return self.me + 1 - 2 * self.core

    def entry(self, extra=()):
        barrier = pltpu.get_barrier_semaphore()
        peers = [{"row": r} for r in (self.row(1, 0), self.row(-1, 0), self.row(0, 1), self.row(0, -1), self.partner())]
        peers += list(extra)
        for peer in peers:
            pl.semaphore_signal(barrier, inc=1, device_id=peer, device_id_type=MESH)
        pl.semaphore_wait(barrier, len(peers))


def push(src, dst, send, recv, row):
    pltpu.make_async_remote_copy(
        src_ref=src, dst_ref=dst, send_sem=send, recv_sem=recv, device_id={"row": row}, device_id_type=MESH
    ).start()


def await_bytes(ref, sem):
    pltpu.make_async_copy(ref, ref, sem).wait()


def gather(place, buf, own, send, recv, pair):
    axes = (("x", "z"), ("z", "x"))

    def owner(g, o1, o2):
        return place.row(o1, o2) if g == 0 else place.row(o2, o1)

    def piece(g, o1, o2, q0, q1):
        dst = buf.at[owner(g, o1, o2), 2 * g + q0 : 2 * g + q1]
        if (o1, o2) == (0, 0):
            return own.at[2 * g + q0 : 2 * g + q1], dst
        return dst, dst

    def slot(g, phase, o1, k):
        ring = 0 if phase == 1 else 1 + OFFSETS.index(o1)
        return recv.at[(g * 5 + ring) * 3 + k]

    def ring_send(g, phase, o1):
        src, dst = piece(g, o1, 0, 0, 2)
        for d, k in ((1, 0), (-1, 1)):
            push(src, dst, send, slot(g, phase, o1, k), place.along(axes[g][phase - 1], d))

    def to_partner(g, o1, o2):
        src, dst = piece(g, o1, o2, 0, 2)
        push(src, dst, send, pair, place.partner())

    def arrived(g, phase, o1, side):
        at = (side, 0) if phase == 1 else (o1, side)
        _, whole = piece(g, at[0], at[1], 0, 2)
        k = 0 if side == -1 else 1
        await_bytes(whole, slot(g, phase, o1, k))
        _, part = piece(g, at[0], at[1], k, k + 1)
        push(part, part, send, slot(g, phase, o1, 2), place.along(axes[g][phase - 1], -side))
        if phase == 1:
            ring_send(g, 2, side)
        to_partner(g, *at)

    def far(g, phase, o1):
        at = (2, 0) if phase == 1 else (o1, 2)
        _, whole = piece(g, at[0], at[1], 0, 2)
        await_bytes(whole, slot(g, phase, o1, 2))
        if phase == 1:
            ring_send(g, 2, 2)
        to_partner(g, *at)

    for g in (0, 1):
        ring_send(g, 1, 0)
    for g in (0, 1):
        ring_send(g, 2, 0)
        to_partner(g, 0, 0)
    yield
    events = []
    for side in (-1, 1):
        events += [(arrived, g, 1, 0, side) for g in (0, 1)]
    for side in (-1, 1):
        events += [(arrived, g, 2, 0, side) for g in (0, 1)]
    events += [(far, g, 1, 0) for g in (0, 1)]
    for o1 in (-1, 1):
        for side in (-1, 1):
            events += [(arrived, g, 2, o1, side) for g in (0, 1)]
    events += [(far, g, 2, 0) for g in (0, 1)]
    for side in (-1, 1):
        events += [(arrived, g, 2, 2, side) for g in (0, 1)]
    for o1 in (-1, 1, 2):
        events += [(far, g, 2, o1) for g in (0, 1)]
    for event in events:
        event[0](*event[1:])
        yield
    await_bytes(buf.at[0:16], pair)
    await_bytes(buf.at[0:31], send)
    yield


def reduce(place, s, t1, t2, t3, t4, out, send, recv):
    axes = (("x", "z"), ("z", "x"))

    def coord(axis, d):
        return lax.rem((place.x if axis == "x" else place.z) + (d + 4), 4)

    def line(g, d, q):
        a = coord(axes[g][0], d)
        return (a, slice(None), q) if g == 0 else (slice(None), a, q)

    def cell(g, d, q):
        a = coord(axes[g][0], 0)
        b = coord(axes[g][1], d)
        return (a, b, q) if g == 0 else (b, a, q)

    def both(g):
        return slice(2 * g, 2 * g + 2)

    def slot(g, k):
        return recv.at[g * 8 + k]

    for phase, index, ta, tb in ((0, line, t1, t2), (1, cell, t3, t4)):
        for g in (0, 1):
            axis = axes[g][phase]
            for k, d in ((0, -1), (1, 1)):
                push(s.at[index(g, 2 * d, 2 * g + k)], ta.at[g, k], send, slot(g, 4 * phase + k), place.along(axis, d))
        yield
        for g in (0, 1):
            axis = axes[g][phase]
            for k, d in ((0, -1), (1, 1)):
                await_bytes(ta.at[g, k], slot(g, 4 * phase + k))
                at = index(g, d, 2 * g + k)
                s[at] = (s[at].astype(F32) + ta[g, k].astype(F32)).astype(BF16)
                push(s.at[index(g, d, both(g))], tb.at[g, k], send, slot(g, 4 * phase + 2 + k), place.along(axis, d))
            yield
        for g in (0, 1):
            for k in (0, 1):
                await_bytes(tb.at[g, k], slot(g, 4 * phase + 2 + k))
            at = index(g, 0, both(g))
            total = s[at].astype(F32) + tb[g, 0].astype(F32) + tb[g, 1].astype(F32)
            if phase == 0:
                s[at] = total.astype(BF16)
            else:
                out[both(g)] = total.astype(BF16)
            yield


def couple(place, c_ref, z_ref, p_send, q_recv, s, send, recv, rows, per_node, pieces):
    step = 16 // pieces

    def product(owner):
        node = owner // per_node
        first = pl.multiple_of(lax.rem(owner, per_node) * rows, rows)
        return jnp.dot(c_ref[node, pl.ds(first, rows), :], z_ref[node], preferred_element_type=F32)

    shape = p_send.shape[1:]
    for piece in range(pieces):

        @pl.loop(piece * step, piece * step + step)
        def _(chip):
            p_send[chip] = product(chip * 2 + 1 - place.core).astype(BF16).reshape(shape)
            push(p_send.at[chip], q_recv.at[chip], send, recv.at[chip], place.partner())

        yield
    for piece in range(pieces):

        @pl.loop(piece * step, piece * step + step)
        def _(chip):
            await_bytes(q_recv.at[chip], recv.at[chip])
            other = q_recv[chip].reshape(rows, shape[2]).astype(F32)
            s[chip // 4, lax.rem(chip, 4)] = (product(chip * 2 + place.core) + other).astype(BF16).reshape(shape)

        yield


def drain(*tasks):
    for task in tasks:
        for _ in task:
            pass


def advance(task, count):
    for _ in range(count):
        if next(task, 0) == 0:
            return


def leaf_kernel(
    load_leaf, load_branch, inverse, coupling, a_branch,
    field, field_branch, u_all,
    b, bb, a, ab, c, z, p_send, q_recv, s, t1, t2, t3, t4, u_own,
    send, recv_l, recv_b, recv_u, pair, recv_s, recv_q, local,
):
    place = Place()
    me = place.me
    width = b.shape[3]
    copies = [
        pltpu.make_async_copy(inverse, a, local.at[0]),
        pltpu.make_async_copy(coupling, c, local.at[1]),
        pltpu.make_async_copy(load_leaf, b.at[me], local.at[2]),
        pltpu.make_async_copy(load_branch, bb.at[me], local.at[3]),
        pltpu.make_async_copy(a_branch, ab, local.at[4]),
    ]
    for copy in copies:
        copy.start()
    place.entry()
    ag_leaf = gather(place, b, load_leaf, send.at[0], recv_l, pair.at[0])
    ag_branch = gather(place, bb, load_branch, send.at[1], recv_b, pair.at[1])
    ag_u = gather(place, u_all, u_own, send.at[2], recv_u, pair.at[2])
    advance(ag_leaf, 27)
    advance(ag_branch, 1)
    for copy in copies[:3]:
        copy.wait()
    drain(ag_leaf)

    def leaf():
        for n in range(4):
            field[n] = jnp.zeros_like(field.at[n])

            @pl.loop(0, place.chip // 4 + 1)
            def _(j):
                cols = pl.ds(pl.multiple_of(j * 1024, 1024), 1024)
                rows = b[pl.ds(j * 8, 8), n].reshape(1024, width)
                field[n] += jnp.dot(a[n, :, cols], rows, preferred_element_type=F32)

            z[n] = field[n].astype(BF16)
            yield
        yield from couple(place, c, z, p_send, q_recv, s, send.at[3], recv_q, 256, 8, 4)

    def branch():
        trips = me // 4 + 1
        copies[3].wait()
        copies[4].wait()
        field_branch[...] = jnp.zeros_like(field_branch)
        for h in range(4):
            for n in range(2):

                @pl.loop(jnp.minimum(trips, 2 * h), jnp.minimum(trips, 2 * h + 2))
                def _(j):
                    cols = pl.ds(pl.multiple_of(j * 1024, 1024), 1024)
                    rows = bb[pl.ds(j * 4, 4), 2 * n : 2 * n + 2].reshape(1024, width)
                    field_branch[n] += jnp.dot(ab[n, :, cols], rows, preferred_element_type=F32)

                yield

    for _ in leaf():
        advance(ag_branch, 1)
    rs = reduce(place, s, t1, t2, t3, t4, u_own, send.at[3], recv_s)
    for _ in rs:
        advance(ag_branch, 2)
    mine = pltpu.make_async_copy(u_own, u_all.at[me], local.at[5])
    mine.start()
    advance(ag_u, 1)
    drain(ag_branch)
    work = branch()
    for _ in ag_u:
        advance(work, 1)
    drain(work)
    await_bytes(u_all.at[0:31], send.at[3])
    mine.wait()


def correct(out, index, a_cols, ids, u_rows, ag):
    for k in range(8):
        ag[:, k * 128 : k * 128 + 128] = a_cols(pl.multiple_of(ids(k) * 128, 128))
    out[index] -= jnp.dot(ag[...], u_rows.reshape(1024, u_rows.shape[-1]), preferred_element_type=F32)


def branch_kernel(
    blocks_leaf, blocks_branch, parents, a_branch, a_root, u_all, partial,
    field, z, root_cols,
    ab, ar, ul, ag, sems,
):
    copies = [pltpu.make_async_copy(a_root, ar, sems.at[5]), pltpu.make_async_copy(a_branch, ab, sems.at[4])]
    for i in range(4):
        copies.append(pltpu.make_async_copy(u_all.at[8 * i : 8 * i + 4], ul.at[i], sems.at[i]))
    for copy in copies:
        copy.start()
    field[...] = partial[...]
    copies[0].wait()
    blocks = [blocks_leaf[i, 8 + k] - 64 for i in range(4) for k in range(8)]
    blocks += [blocks_branch[p, k] for p in range(2) for k in range(16)]
    for slot, block in enumerate(blocks):
        root_cols[:, slot * 128 : slot * 128 + 128] = ar[:, pl.ds(pl.multiple_of(block * 128, 128), 128)]
    for copy in copies[1:]:
        copy.wait()

    @pl.loop(0, 4)
    def _(i):
        n = parents[i]
        correct(field, n, lambda col: ab[n, :, pl.ds(col, 128)], lambda k: blocks_leaf[i, k], ul[i], ag)

    z[...] = field[...].astype(BF16)


def upper_kernel(
    z_in, c_branch, a_root, load_root, root_cols, u_all,
    field_root,
    zb, cb, ar, br, cols_root, ul, u2, p_send, q_recv, s, t1, t2, t3, t4, u_own,
    send, recv_r, recv_u, pair, recv_s, recv_q, local,
):
    place = Place()
    me = place.me
    width = br.shape[3]
    pairs = ((z_in, zb), (c_branch, cb), (load_root, br.at[me]), (a_root, ar), (root_cols, cols_root))
    copies = [pltpu.make_async_copy(src, dst, local.at[k]) for k, (src, dst) in enumerate(pairs)]
    for i in range(4):
        copies.append(pltpu.make_async_copy(u_all.at[8 * i + 4 : 8 * i + 8], ul.at[i], local.at[6 + i]))
    for copy in copies:
        copy.start()
    place.entry()
    ag_root = gather(place, br, load_root, send.at[2], recv_r, pair.at[1])
    advance(ag_root, 1)
    copies[0].wait()
    copies[1].wait()
    for _ in couple(place, cb, zb, p_send, q_recv, s, send.at[0], recv_q, 128, 16, 4):
        advance(ag_root, 1)

    def root():
        trips = me // 4 + 1
        copies[2].wait()
        copies[3].wait()
        field_root[...] = jnp.zeros_like(field_root)
        for h in range(4):

            @pl.loop(jnp.minimum(trips, 2 * h), jnp.minimum(trips, 2 * h + 2))
            def _(j):
                cols = pl.ds(pl.multiple_of(j * 1024, 1024), 1024)
                rows = br[pl.ds(j * 4, 4)].reshape(1024, width)
                field_root[...] += jnp.dot(ar[:, cols], rows, preferred_element_type=F32)

            yield
        for copy in copies[4:]:
            copy.wait()
        for i in range(4):
            correct(i, ul[i])
            yield

    def correct(chunk, u_rows):
        cols = cols_root[:, chunk * 1024 : chunk * 1024 + 1024]
        field_root[...] -= jnp.dot(cols, u_rows.reshape(1024, width), preferred_element_type=F32)

    rs = reduce(place, s, t1, t2, t3, t4, u_own, send.at[0], recv_s)
    for _ in rs:
        advance(ag_root, 2)
    mine = pltpu.make_async_copy(u_own, u2.at[me], local.at[5])
    mine.start()
    ag_u = gather(place, u2, u_own, send.at[1], recv_u, pair.at[0])
    advance(ag_u, 1)
    drain(ag_root)
    work = root()
    for _ in ag_u:
        advance(work, 1)
    drain(work)
    mine.wait()
    for q in range(4):
        correct(4 + q, u2[8 * q : 8 * q + 8])
    await_bytes(u2.at[0:31], send.at[0])


def reduce_scratch(q, c):
    return [
        pltpu.VMEM((16, 4, q, c), BF16),
        pltpu.VMEM((16, 4, q, c), BF16),
        pltpu.VMEM((4, 4, 4, q, c), BF16),
        pltpu.VMEM((2, 2, 4, q, c), BF16),
        pltpu.VMEM((2, 2, 4, 2, q, c), BF16),
        pltpu.VMEM((2, 2, q, c), BF16),
        pltpu.VMEM((2, 2, 2, q, c), BF16),
        pltpu.VMEM((4, q, c), BF16),
    ]


def local(
    load_root, load_branch, load_leaf, inverse_root, inverse_branch, inverse_leaf,
    coupling_branch, coupling_leaf, blocks_branch, blocks_leaf, parents,
):
    c = load_leaf.shape[2]
    dma = pltpu.SemaphoreType.DMA
    anywhere = pl.BlockSpec(memory_space=pl.ANY)
    vmem = pl.BlockSpec(memory_space=pltpu.VMEM)
    smem = pl.BlockSpec(memory_space=pltpu.SMEM)
    field_leaf, partial_branch, u_all = pl.pallas_call(
        leaf_kernel,
        out_shape=(
            jax.ShapeDtypeStruct((4, 128, c), F32),
            jax.ShapeDtypeStruct((2, 256, c), F32),
            jax.ShapeDtypeStruct((32, 4, 64, c), BF16),
        ),
        in_specs=[anywhere] * 5,
        out_specs=(vmem, vmem, anywhere),
        scratch_shapes=[
            pltpu.VMEM((32, 4, 128, c), BF16),
            pltpu.VMEM((32, 4, 128, c), BF16),
            pltpu.VMEM((4, 128, 4096), BF16),
            pltpu.VMEM((2, 256, 8192), BF16),
            pltpu.VMEM((4, 2048, 128), BF16),
            pltpu.VMEM((4, 128, c), BF16),
            *reduce_scratch(64, c),
            dma((4,)), dma((30,)), dma((30,)), dma((30,)), dma((3,)), dma((16,)), dma((16,)), dma((6,)),
        ],
        compiler_params=pltpu.CompilerParams(
            collective_id=0, has_side_effects=True, vmem_limit_bytes=62 * 1024 * 1024
        ),
        name="leaf_level",
    )(load_leaf, load_branch.reshape(4, 128, c), inverse_leaf, coupling_leaf, inverse_branch)
    field_branch, z_branch, root_cols = pl.pallas_call(
        branch_kernel,
        out_shape=(
            jax.ShapeDtypeStruct((2, 256, c), F32),
            jax.ShapeDtypeStruct((2, 256, c), BF16),
            jax.ShapeDtypeStruct((256, 8192), BF16),
        ),
        in_specs=[smem] * 3 + [anywhere] * 3 + [vmem],
        out_specs=(vmem, vmem, vmem),
        scratch_shapes=[
            pltpu.VMEM((2, 256, 8192), BF16),
            pltpu.VMEM((256, 8192), BF16),
            pltpu.VMEM((4, 4, 4, 64, c), BF16),
            pltpu.VMEM((256, 1024), BF16),
            dma((6,)),
        ],
        compiler_params=pltpu.CompilerParams(vmem_limit_bytes=60 * 1024 * 1024),
        name="branch_level",
    )(blocks_leaf, blocks_branch, parents, inverse_branch, inverse_root, u_all, partial_branch)
    field_root = pl.pallas_call(
        upper_kernel,
        out_shape=jax.ShapeDtypeStruct((256, c), F32),
        in_specs=[anywhere] * 6,
        out_specs=vmem,
        scratch_shapes=[
            pltpu.VMEM((2, 256, c), BF16),
            pltpu.VMEM((2, 2048, 256), BF16),
            pltpu.VMEM((256, 8192), BF16),
            pltpu.VMEM((32, 4, 64, c), BF16),
            pltpu.VMEM((256, 8192), BF16),
            pltpu.VMEM((4, 4, 4, 64, c), BF16),
            pltpu.VMEM((32, 4, 32, c), BF16),
            *reduce_scratch(32, c),
            dma((3,)), dma((30,)), dma((30,)), dma((2,)), dma((16,)), dma((16,)), dma((10,)),
        ],
        compiler_params=pltpu.CompilerParams(
            collective_id=1, has_side_effects=True, vmem_limit_bytes=60 * 1024 * 1024
        ),
        name="root_level",
    )(z_branch, coupling_branch, inverse_root, load_root.reshape(4, 64, c), root_cols, u_all)
    coverage_root, coverage_branch, coverage_leaf = lax.psum(
        (
            jnp.sum(field_root * field_root, axis=-1),
            jnp.sum(field_branch * field_branch, axis=-1),
            jnp.sum(field_leaf * field_leaf, axis=-1),
        ),
        "src",
    )
    return (field_root, field_branch, field_leaf, coverage_root, coverage_branch, coverage_leaf)


def solution(mesh):
    return jax.shard_map(
        local,
        mesh=mesh,
        in_specs=(
            P("row", "src"),
            P(None, "row", "src"),
            P(None, "row", "src"),
            P("row", None),
            P(None, "row", None),
            P(None, "row", None),
            P(None, None, "row"),
            P(None, None, "row"),
            P(),
            P(),
            P(),
        ),
        out_specs=(
            P("row", "src"),
            P(None, "row", "src"),
            P(None, "row", "src"),
            P("row"),
            P(None, "row"),
            P(None, "row"),
        ),
        check_vma=False,
    )
```
